32 devices in a mesh: groups: 2 (over y), ep: 8 (over z, x), tp: 2 (over core).
Axes of the slice: x: 2, y: 2, z: 4, core: 2. Of those that a mesh axis runs over, the one named last changes fastest.
Arguments:
- hidden: bfloat16 [128, 4096], P(('groups', 'ep', 'tp')), parts along dimension 0, may hold values from -6 to 6
- norm_gain: float32 [4096], replicated, may hold values from 0.5 to 1.5
- rot_left: float32 [64, 64], replicated, may hold values from -0.75 to 0.75
- rot_right: float32 [64, 64], replicated, may hold values from -0.75 to 0.75
- expert_ids: int32 [128, 8], P(('groups', 'ep')), parts along dimension 0, may hold values from 0 to 63, as said below
- gate_weights: float32 [128, 8], P(('groups', 'ep')), parts along dimension 0, may hold values from 0.05 to 1
- w_gate: bfloat16 [128, 4096, 384], P('ep', 'tp'), may hold values from -0.09375 to 0.09375
- w_up: bfloat16 [128, 4096, 384], P('ep', 'tp'), may hold values from -0.09375 to 0.09375
- w_down: bfloat16 [128, 384, 4096], P('ep', None, 'tp'), may hold values from -0.21875 to 0.21875
- unit_scales: float32 [128, 2, 384], P('ep'), may hold values from 0.25 to 1.75
Outputs:
- moe_out: bfloat16 [128, 4096], P(('groups', 'ep', 'tp')), parts along dimension 0
The draws below stay inside these ranges and needn't reach their ends.
There are 2 independent parts, one for each index of `groups`. The reference program is written for one: setup_inputs(seed, part) draws one part's arguments, and reference() takes and returns one part's arrays. A program takes and returns all parts, laid end to end along the dimension named above; an argument that names none is the same for every part. Nothing has to cross between parts.
Inputs may be any that keep to these rules, and one draw needn't show every extreme that they name: `expert_ids`: each row names 8 different experts. In each aligned block of 8 rows (the rows of one index of ep) no expert is named by more than 2 rows, and in every block some experts are named by exactly 2 rows; every expert is named by exactly 2 rows in some block.
All inputs are finite; a program needn't handle non-finite values.
Results may differ from the reference program's by a relative error of at most 0.0082.
Values may be sent and summed in bfloat16 or wider, within the bound.
A program may use at most 128 MiB of HBM per device.

```python
import math
import jax
import jax.numpy as jnp
from jax import lax

D = 4096
ROT = 64
FF = 768
EXPERTS = 64
TOPK = 8
R_DEV = 4
ROWS = 64
CAP = 2
N_TP = 2


def draw_expert_ids(key, part):
    group_rows = R_DEV * N_TP
    block_count = ROWS // group_rows
    labels = jax.random.permutation(jax.random.fold_in(key, 11), EXPERTS).astype(jnp.int32)
    offset = jax.random.randint(jax.random.fold_in(key, 12), (), 0, EXPERTS, dtype=jnp.int32)
    block_index = jnp.arange(block_count, dtype=jnp.int32)[:, None, None]
    row_index = jnp.arange(group_rows, dtype=jnp.int32)[None, :, None]
    choice_index = jnp.arange(TOPK, dtype=jnp.int32)[None, None, :]
    spot = (block_index * TOPK + row_index // CAP * TOPK + choice_index + offset) % EXPERTS
    chosen = labels[spot]

    def order_of(block):
        return jax.random.permutation(jax.random.fold_in(key, 1000 + block), group_rows).astype(jnp.int32)
    orders = jax.vmap(order_of)(jnp.arange(block_count, dtype=jnp.int32))
    chosen = jnp.take_along_axis(chosen, orders[:, :, None], axis=1)
    return chosen.reshape(ROWS, TOPK).astype(jnp.int32)


def block_levels(stream_key, extent, shards, low, high):
    level = 1.0
    for dim, parts in shards:
        heights = jax.random.uniform(jax.random.fold_in(jax.random.fold_in(stream_key, 6), dim), (parts,), jnp.float32, low / len(shards), high / len(shards))
        level = level * jnp.repeat(jnp.exp(heights), extent[dim] // parts).reshape((-1,) + (1,) * (len(extent) - 1 - dim))
    return level


def gaussian(rng, shape, width, limit, shards=(), kind=jnp.bfloat16):
    entries = jax.random.normal(rng, shape, jnp.float32) * width
    if len(shards) > 0:
        entries = block_levels(rng, shape, shards, -0.22, 0.18) * entries
    return jnp.clip(entries, min=-limit, max=limit).astype(kind)


def setup_inputs(seed: int = 0, part: int = 0) -> dict:
    keys = jax.random.split(jax.random.key(seed), 11)
    part_splits = jax.random.split(jax.random.fold_in(keys[10], part), 11)
    hidden = gaussian(part_splits[0], (ROWS, D), 1.0, 6.0, ((0, 16),))
    norm_gain = jnp.clip(1.0 + 0.1 * jax.random.normal(keys[1], (D,), jnp.float32), 0.5, 1.5)
    rot_left = gaussian(keys[2], (ROT, ROT), ROT ** -0.5, 0.75, (), jnp.float32)
    rot_right = gaussian(keys[3], (ROT, ROT), ROT ** -0.5, 0.75, (), jnp.float32)
    expert_ids = draw_expert_ids(jax.random.fold_in(jax.random.fold_in(keys[10], part), 71), part)
    gate_weights = jnp.clip(jnp.exp(math.log(1.0) - 2.9957323 * jax.random.uniform(part_splits[5], (ROWS, TOPK), jnp.float32) ** block_levels(part_splits[5], (ROWS, TOPK), ((0, 8),), -0.2, 0.2)), 0.05, 1.0)
    w_gate = gaussian(keys[6], (2 * EXPERTS, D, FF // 2), D ** -0.5, 0.09375, ((0, 8), (1, 2)))
    w_up = gaussian(keys[7], (2 * EXPERTS, D, FF // 2), D ** -0.5, 0.09375, ((0, 8), (1, 2)))
    w_down = gaussian(keys[8], (2 * EXPERTS, FF // 2, D), FF ** -0.5, 0.21875, ((0, 8), (2, 2)))
    unit_scales = jnp.clip(1.0 + 0.15 * jax.random.normal(keys[9], (2 * EXPERTS, 2, FF // 2), jnp.float32), 0.25, 1.75)
    return {"hidden": hidden, "norm_gain": norm_gain, "rot_left": rot_left, "rot_right": rot_right, "expert_ids": expert_ids, "gate_weights": gate_weights, "w_gate": w_gate, "w_up": w_up, "w_down": w_down, "unit_scales": unit_scales}


def rotate(hidden, norm_gain, rot_left, rot_right):
    values = hidden.astype(jnp.float32)
    mean_square = lax.optimization_barrier(jnp.mean(values * values, axis=1, keepdims=True))
    normed = values * lax.rsqrt(mean_square + 1e-06) * norm_gain[None, :]
    factor = rot_left.shape[0]
    square = normed.reshape(-1, factor, factor)
    turned = jnp.einsum('ij,rjk->rik', rot_left, square, precision=lax.Precision.HIGHEST)
    turned = jnp.einsum('rik,lk->ril', turned, rot_right, precision=lax.Precision.HIGHEST)
    return turned.reshape(normed.shape).astype(jnp.bfloat16)

def reference(hidden, norm_gain, rot_left, rot_right, expert_ids, gate_weights, w_gate, w_up, w_down, unit_scales):
    row_count = hidden.shape[0]
    group_rows = R_DEV * N_TP
    block_count = row_count // group_rows
    half_ff = w_gate.shape[2]
    rotated = rotate(hidden, norm_gain, rot_left, rot_right)
    weight_norm = (gate_weights / lax.optimization_barrier(jnp.sum(gate_weights, axis=1, keepdims=True))).astype(jnp.bfloat16)
    blocks = expert_ids.reshape(block_count, group_rows * TOPK)
    onehot = (blocks[:, :, None] == jnp.arange(EXPERTS, dtype=jnp.int32)[None, None, :]).astype(jnp.int32)
    slot_rank = lax.optimization_barrier(jnp.sum((jnp.cumsum(onehot, axis=1) - onehot) * onehot, axis=2))
    position = (jnp.arange(block_count, dtype=jnp.int32)[:, None] * group_rows + jnp.arange(group_rows * TOPK, dtype=jnp.int32)[None, :] // TOPK).astype(jnp.int32)
    weight_flat = weight_norm.astype(jnp.float32).reshape(block_count, group_rows * TOPK)
    slot_index = jnp.arange(CAP, dtype=jnp.int32)

    def expert_step(total, expert):
        selects = ((blocks == expert)[:, :, None] & (slot_rank[:, :, None] == slot_index[None, None, :])).astype(jnp.int32)
        gather_index = lax.optimization_barrier(jnp.sum(selects * position[:, :, None], axis=1)).reshape(-1).astype(jnp.int32)
        portion = lax.optimization_barrier(jnp.sum(selects.astype(jnp.float32) * weight_flat[:, :, None], axis=1)).reshape(-1)
        inputs = jnp.take(rotated, gather_index, axis=0)
        gate_full = jnp.concatenate((w_gate[expert], w_gate[EXPERTS + expert]), axis=1)
        up_full = jnp.concatenate((w_up[expert], w_up[EXPERTS + expert]), axis=1)
        gate_scale = jnp.concatenate((unit_scales[expert, 0], unit_scales[EXPERTS + expert, 0]), axis=0)
        up_scale = jnp.concatenate((unit_scales[expert, 1], unit_scales[EXPERTS + expert, 1]), axis=0)
        gate_sum = jnp.dot(inputs, gate_full, preferred_element_type=jnp.float32) * gate_scale[None, :]
        up_sum = jnp.dot(inputs, up_full, preferred_element_type=jnp.float32) * up_scale[None, :]
        hidden_units = (jax.nn.silu(gate_sum) * up_sum).astype(jnp.bfloat16)
        lower_out = jnp.dot(hidden_units[:, :half_ff], w_down[expert], preferred_element_type=jnp.float32).astype(jnp.bfloat16)
        upper_out = jnp.dot(hidden_units[:, half_ff:], w_down[EXPERTS + expert], preferred_element_type=jnp.float32).astype(jnp.bfloat16)
        expert_out = lax.optimization_barrier((lower_out.astype(jnp.float32) + upper_out.astype(jnp.float32)).astype(jnp.bfloat16))
        contribution = portion[:, None] * expert_out.astype(jnp.float32)
        return (total.at[gather_index].add(contribution), None)
    start = jnp.zeros((row_count, hidden.shape[1]), jnp.float32)
    total, _ = lax.scan(expert_step, start, jnp.arange(EXPERTS, dtype=jnp.int32))
    return total.astype(jnp.bfloat16)
```

```python
import functools

import jax
import jax.numpy as jnp
from jax import lax
from jax.experimental import pallas as pl
from jax.experimental.pallas import tpu as pltpu
from jax.sharding import PartitionSpec as P

MESH = pl.DeviceIdType.MESH
HIGH = lax.Precision.HIGHEST
LANES = 128
LAG = 3
UNIT_RING = 10
DOWN_RING = 8


def iota(shape, dim):
    return lax.broadcasted_iota(jnp.int32, shape, dim)


def rotate(hid_ref, gain_ref, left_ref, right_ref, n_tp):
    values = hid_ref[...].astype(jnp.float32)
    rows, width = values.shape
    half = width // n_tp
    order = left_ref.shape[0]
    mean_square = jnp.mean(values * values, axis=1, keepdims=True)
    normed = values * lax.rsqrt(mean_square + 1e-06) * gain_ref[...]
    stacked = jnp.concatenate([normed[:, h * half : (h + 1) * half] for h in range(n_tp)], axis=0)
    groups = half // LANES
    tall = jnp.concatenate(
        [stacked[:, m * LANES : (m + 1) * LANES] for m in range(groups)], axis=0
    )
    per_lane = LANES // order
    tall = jnp.concatenate(
        [tall[:, p * order : (p + 1) * order] for p in range(per_lane)], axis=0
    )
    count = tall.shape[0]
    block = n_tp * rows

    def line_of(index):
        return (
            (index % block) // rows * (half // order)
            + index // block % groups * per_lane
            + index // (block * groups)
        )

    spread = (line_of(iota((count, order), 0)) == iota((count, order), 1)).astype(jnp.float32)
    dims = (((1,), (1,)), ((), ()))
    wide = lax.dot_general(
        jnp.dot(spread, left_ref[...], precision=HIGH, preferred_element_type=jnp.float32),
        spread,
        dims,
        precision=HIGH,
        preferred_element_type=jnp.float32,
    )
    same_row = iota((count, count), 0) % rows == iota((count, count), 1) % rows
    wide = jnp.where(same_row, wide, 0.0)
    turned = lax.dot_general(
        tall, right_ref[...], dims, precision=HIGH, preferred_element_type=jnp.float32
    )
    turned = jnp.dot(wide, turned, precision=HIGH, preferred_element_type=jnp.float32)
    step = count // per_lane
    flat = jnp.concatenate([turned[p * step : (p + 1) * step] for p in range(per_lane)], axis=1)
    return jnp.concatenate([flat[m * block : (m + 1) * block] for m in range(groups)], axis=1)


def routing(ids_ref, weights_ref, experts, capacity):
    ids = ids_ref[...]
    weights = weights_ref[...]
    rows, choices = ids.shape
    weights = weights / jnp.sum(weights, axis=1, keepdims=True)
    weights = weights.astype(jnp.bfloat16).astype(jnp.float32)
    lane = iota((rows, capacity * experts), 1)
    expert = lane % experts
    named = jnp.zeros(lane.shape, jnp.float32)
    value = jnp.zeros(lane.shape, jnp.float32)
    for k in range(choices):
        hit = (ids[:, k : k + 1] == expert).astype(jnp.float32)
        named = named + hit
        value = value + hit * weights[:, k : k + 1]
    row = iota(lane.shape, 0)
    rank = jnp.zeros(lane.shape, jnp.float32)
    for r in range(rows):
        rank = rank + jnp.where(row > r, named[r : r + 1, :], 0.0)
    return jnp.where(rank == (lane // experts).astype(jnp.float32), value, 0.0)


def kernel(
    sizes,
    hid_ref,
    gain_ref,
    left_ref,
    right_ref,
    ids_ref,
    weights_ref,
    scales_ref,
    gate_hbm,
    up_hbm,
    down_hbm,
    out_ref,
    gate_buf,
    up_buf,
    down_buf,
    row_out,
    row_in,
    route_out,
    route_in,
    rows_f32,
    route_t,
    lines,
    part_out,
    part_in,
    values,
    back_out,
    back_in,
    gate_sem,
    up_sem,
    down_sem,
    part_send,
    part_recv,
    plain_sem,
):
    n_ep, n_tp, capacity = sizes
    peers = n_ep * n_tp
    ep = lax.axis_index("ep")
    tp = lax.axis_index("tp")
    me = ep * n_tp + tp
    held = gate_hbm.shape[0]
    unit_ring = gate_buf.shape[0]
    down_ring = down_buf.shape[0]
    rows = hid_ref.shape[0]
    half = row_in.shape[2]
    block = rows * n_tp
    slots = capacity * n_ep
    ff = gate_hbm.shape[2]
    experts = held * n_ep // 2
    total_rows = n_ep * block

    def unit_copies(j, slot):
        return (
            pltpu.make_async_copy(gate_hbm.at[j], gate_buf.at[slot], gate_sem.at[slot]),
            pltpu.make_async_copy(up_hbm.at[j], up_buf.at[slot], up_sem.at[slot]),
        )

    def down_copy(j, slot):
        return pltpu.make_async_copy(down_hbm.at[j], down_buf.at[slot], down_sem.at[slot])

    for j in range(max(unit_ring, down_ring + LAG)):
        if j < unit_ring:
            for copy in unit_copies(j, j):
                copy.start()
        if LAG <= j < down_ring + LAG:
            down_copy(j - LAG, j - LAG).start()

    barrier = pltpu.get_barrier_semaphore()

    def peer_of(offset):
        peer = lax.rem(me + offset, peers)
        return {"ep": peer // n_tp, "tp": lax.rem(peer, n_tp)}, peer

    @pl.loop(1, peers)
    def _(offset):
        where, _peer = peer_of(offset)
        pl.semaphore_signal(barrier, inc=1, device_id=where, device_id_type=MESH)

    route = routing(ids_ref, weights_ref, experts, capacity)
    route_out[...] = route
    route_in[ep] = route
    rotated = rotate(hid_ref, gain_ref, left_ref, right_ref, n_tp).astype(jnp.float32)
    for h in range(n_tp):
        row_out[h] = rotated[h * rows : (h + 1) * rows].astype(jnp.bfloat16)
    row_in[me] = row_out[tp]

    pl.semaphore_wait(barrier, peers - 1)

    @pl.loop(1, n_ep)
    def _(offset):
        pltpu.make_async_remote_copy(
            src_ref=route_out,
            dst_ref=route_in.at[ep],
            send_sem=plain_sem.at[0],
            recv_sem=plain_sem.at[1],
            device_id={"ep": lax.rem(ep + offset, n_ep), "tp": tp},
            device_id_type=MESH,
        ).start()

    @pl.loop(1, peers)
    def _(offset):
        where, peer = peer_of(offset)
        pltpu.make_async_remote_copy(
            src_ref=row_out.at[lax.rem(peer, n_tp)],
            dst_ref=row_in.at[me],
            send_sem=plain_sem.at[2],
            recv_sem=plain_sem.at[3],
            device_id=where,
            device_id_type=MESH,
        ).start()

    def drain(ref, count, sem):
        view = ref.at[pl.ds(0, count)]
        pltpu.make_async_copy(view, view, sem).wait()

    drain(route_in, n_ep - 1, plain_sem.at[1])
    route_t[...] = route_in[...].reshape(total_rows, capacity * experts).T
    first = lax.rem(ep * held, experts)
    owner = (iota((n_ep, total_rows), 1) // block == iota((n_ep, total_rows), 0)).astype(jnp.float32)
    picks = []
    for c in range(capacity):
        line = route_t[pl.ds(c * experts + first, held), :]
        picks.append((line[:, None, :] * owner[None, :, :])[:, None])
    weighted = jnp.concatenate(picks, axis=1).reshape(held * slots, total_rows)
    chosen = jnp.where(weighted > 0.0, 1.0, 0.0).astype(jnp.bfloat16)
    mixing = weighted.T.astype(jnp.bfloat16)

    drain(row_in, peers - 1, plain_sem.at[3])

    @pl.loop(0, n_ep)
    def _(b):
        both = [row_in[b * n_tp + h].astype(jnp.float32) for h in range(n_tp)]
        rows_f32[pl.ds(pl.multiple_of(b * block, block), block), :] = jnp.concatenate(both, axis=0)

    lines[...] = (
        jnp.dot(chosen, rows_f32[...].astype(jnp.bfloat16), preferred_element_type=jnp.float32)
        .astype(jnp.bfloat16)
        .reshape(lines.shape)
    )

    def part_copy(j):
        return pltpu.make_async_remote_copy(
            src_ref=part_out.at[j],
            dst_ref=part_in.at[j],
            send_sem=part_send.at[j],
            recv_sem=part_recv.at[j],
            device_id={"ep": ep, "tp": 1 - tp},
            device_id_type=MESH,
        )

    @pl.loop(0, held + LAG)
    def _(t):
        @pl.when(t < held)
        def _():
            slot = lax.rem(t, unit_ring)
            for copy in unit_copies(t, slot):
                copy.wait()
            line = lines[t]
            part_out[t, :, pl.ds(0, ff)] = jnp.dot(
                line, gate_buf[slot], preferred_element_type=jnp.float32
            )
            part_out[t, :, pl.ds(ff, ff)] = jnp.dot(
                line, up_buf[slot], preferred_element_type=jnp.float32
            )
            part_copy(t).start()

            @pl.when(t + unit_ring < held)
            def _():
                for copy in unit_copies(t + unit_ring, slot):
                    copy.start()

        @pl.when(t >= LAG)
        def _():
            j = t - LAG
            slot = lax.rem(j, down_ring)
            part_copy(j).wait_recv()
            scale = scales_ref[j]
            gate = (part_out[j, :, pl.ds(0, ff)] + part_in[j, :, pl.ds(0, ff)]) * scale[0:1]
            up = (part_out[j, :, pl.ds(ff, ff)] + part_in[j, :, pl.ds(ff, ff)]) * scale[1:2]
            units = (gate / (1.0 + jnp.exp(-gate)) * up).astype(jnp.bfloat16)
            down_copy(j, slot).wait()
            values[pl.ds(pl.multiple_of(j * slots, slots), slots), :] = jnp.dot(
                units, down_buf[slot], preferred_element_type=jnp.float32
            ).astype(jnp.bfloat16)

            @pl.when(j + down_ring < held)
            def _():
                down_copy(j + down_ring, slot).start()

    rows_f32[...] = jnp.dot(mixing, values[...], preferred_element_type=jnp.float32)

    @pl.loop(0, n_ep)
    def _(b):
        both = rows_f32[pl.ds(pl.multiple_of(b * block, block), block), :]
        for h in range(n_tp):
            back_out[b * n_tp + h] = both[h * rows : (h + 1) * rows].astype(jnp.bfloat16)

    back_in[me] = back_out[me]

    @pl.loop(1, peers)
    def _(offset):
        where, peer = peer_of(offset)
        pltpu.make_async_remote_copy(
            src_ref=back_out.at[peer],
            dst_ref=back_in.at[me],
            send_sem=plain_sem.at[4],
            recv_sem=plain_sem.at[5],
            device_id=where,
            device_id_type=MESH,
        ).start()

    @pl.loop(0, held)
    def _(j):
        part_copy(j).wait_send()

    drain(route_in, n_ep - 1, plain_sem.at[0])
    drain(row_in, peers - 1, plain_sem.at[2])
    drain(back_in, peers - 1, plain_sem.at[5])
    for h in range(n_tp):
        def add(e, total):
            return total + back_in[e * n_tp + h].astype(jnp.float32)

        total = lax.fori_loop(0, n_ep, add, jnp.zeros((rows, half), jnp.float32))
        out_ref[:, h * half : (h + 1) * half] = total.astype(jnp.bfloat16)
    drain(back_in, peers - 1, plain_sem.at[4])


def body(
    hidden,
    norm_gain,
    rot_left,
    rot_right,
    expert_ids,
    gate_weights,
    w_gate,
    w_up,
    w_down,
    unit_scales,
):
    n_ep, n_tp = lax.axis_size("ep"), lax.axis_size("tp")
    peers = n_ep * n_tp
    rows, width = hidden.shape
    group_rows, choices = expert_ids.shape
    held, half, ff = w_gate.shape
    experts = held * n_ep // 2
    capacity = 5 * group_rows * choices // (2 * experts)
    slots = capacity * n_ep
    total_rows = n_ep * group_rows
    unit_ring, down_ring = min(UNIT_RING, held), min(DOWN_RING, held)
    vmem = pl.BlockSpec(memory_space=pltpu.VMEM)
    hbm = pl.BlockSpec(memory_space=pl.ANY)
    return pl.pallas_call(
        functools.partial(kernel, (n_ep, n_tp, capacity)),
        out_shape=jax.ShapeDtypeStruct((rows, width), jnp.bfloat16),
        in_specs=[vmem] * 7 + [hbm] * 3,
        out_specs=vmem,
        scratch_shapes=[
            pltpu.VMEM((unit_ring, half, ff), jnp.bfloat16),
            pltpu.VMEM((unit_ring, half, ff), jnp.bfloat16),
            pltpu.VMEM((down_ring, ff, half), jnp.bfloat16),
            pltpu.VMEM((n_tp, rows, half), jnp.bfloat16),
            pltpu.VMEM((peers, rows, half), jnp.bfloat16),
            pltpu.VMEM((group_rows, capacity * experts), jnp.float32),
            pltpu.VMEM((n_ep, group_rows, capacity * experts), jnp.float32),
            pltpu.VMEM((total_rows, half), jnp.float32),
            pltpu.VMEM((capacity * experts, total_rows), jnp.float32),
            pltpu.VMEM((held, slots, half), jnp.bfloat16),
            pltpu.VMEM((held, slots, 2 * ff), jnp.float32),
            pltpu.VMEM((held, slots, 2 * ff), jnp.float32),
            pltpu.VMEM((held * slots, half), jnp.bfloat16),
            pltpu.VMEM((peers, rows, half), jnp.bfloat16),
            pltpu.VMEM((peers, rows, half), jnp.bfloat16),
            pltpu.SemaphoreType.DMA((unit_ring,)),
            pltpu.SemaphoreType.DMA((unit_ring,)),
            pltpu.SemaphoreType.DMA((down_ring,)),
            pltpu.SemaphoreType.DMA((held,)),
            pltpu.SemaphoreType.DMA((held,)),
            pltpu.SemaphoreType.DMA((6,)),
        ],
        compiler_params=pltpu.CompilerParams(
            collective_id=0, has_side_effects=True, vmem_limit_bytes=62 * 1024 * 1024
        ),
    )(
        hidden,
        norm_gain.reshape(1, width),
        rot_left,
        rot_right,
        expert_ids,
        gate_weights,
        unit_scales,
        w_gate,
        w_up,
        w_down,
    )


def solution(mesh):
    placed = (
        P(("groups", "ep", "tp"), None),
        P(),
        P(),
        P(),
        P(("groups", "ep"), None),
        P(("groups", "ep"), None),
        P("ep", "tp", None),
        P("ep", "tp", None),
        P("ep", None, "tp"),
        P("ep", None, None),
    )
    return jax.shard_map(
        body, mesh=mesh, in_specs=placed, out_specs=P(("groups", "ep", "tp"), None), check_vma=False
    )
```

```python
import functools

import jax
import jax.numpy as jnp
from jax import lax
from jax.experimental import pallas as pl
from jax.experimental.pallas import tpu as pltpu
from jax.sharding import PartitionSpec as P

MESH = pl.DeviceIdType.MESH
HIGH = lax.Precision.HIGHEST
LANES = 128
LAG = 3
UNIT_RING = 10
CHUNK = 512


def iota(shape, dim):
    return lax.broadcasted_iota(jnp.int32, shape, dim)


def rotate(hid_ref, gain_ref, left_ref, right_ref, n_tp):
    values = hid_ref[...].astype(jnp.float32)
    rows, width = values.shape
    half = width // n_tp
    order = left_ref.shape[0]
    mean_square = jnp.mean(values * values, axis=1, keepdims=True)
    normed = values * lax.rsqrt(mean_square + 1e-06) * gain_ref[...]
    stacked = jnp.concatenate([normed[:, h * half : (h + 1) * half] for h in range(n_tp)], axis=0)
    groups = half // LANES
    tall = jnp.concatenate(
        [stacked[:, m * LANES : (m + 1) * LANES] for m in range(groups)], axis=0
    )
    per_lane = LANES // order
    tall = jnp.concatenate(
        [tall[:, p * order : (p + 1) * order] for p in range(per_lane)], axis=0
    )
    count = tall.shape[0]
    block = n_tp * rows

    def line_of(index):
        return (
            (index % block) // rows * (half // order)
            + index // block % groups * per_lane
            + index // (block * groups)
        )

    spread = (line_of(iota((count, order), 0)) == iota((count, order), 1)).astype(jnp.float32)
    dims = (((1,), (1,)), ((), ()))
    wide = lax.dot_general(
        jnp.dot(spread, left_ref[...], precision=HIGH, preferred_element_type=jnp.float32),
        spread,
        dims,
        precision=HIGH,
        preferred_element_type=jnp.float32,
    )
    same_row = iota((count, count), 0) % rows == iota((count, count), 1) % rows
    wide = jnp.where(same_row, wide, 0.0)
    turned = lax.dot_general(
        tall, right_ref[...], dims, precision=HIGH, preferred_element_type=jnp.float32
    )
    turned = jnp.dot(wide, turned, precision=HIGH, preferred_element_type=jnp.float32)
    step = count // per_lane
    flat = jnp.concatenate([turned[p * step : (p + 1) * step] for p in range(per_lane)], axis=1)
    return jnp.concatenate([flat[m * block : (m + 1) * block] for m in range(groups)], axis=1)


def routing(ids_ref, weights_ref, experts, capacity):
    ids = ids_ref[...]
    weights = weights_ref[...]
    rows, choices = ids.shape
    weights = weights / jnp.sum(weights, axis=1, keepdims=True)
    weights = weights.astype(jnp.bfloat16).astype(jnp.float32)
    lane = iota((rows, capacity * experts), 1)
    expert = lane % experts
    named = jnp.zeros(lane.shape, jnp.float32)
    value = jnp.zeros(lane.shape, jnp.float32)
    for k in range(choices):
        hit = (ids[:, k : k + 1] == expert).astype(jnp.float32)
        named = named + hit
        value = value + hit * weights[:, k : k + 1]
    row = iota(lane.shape, 0)
    rank = jnp.zeros(lane.shape, jnp.float32)
    for r in range(rows):
        rank = rank + jnp.where(row > r, named[r : r + 1, :], 0.0)
    return jnp.where(rank == (lane // experts).astype(jnp.float32), value, 0.0)


def kernel(
    sizes,
    hid_ref,
    gain_ref,
    left_ref,
    right_ref,
    ids_ref,
    weights_ref,
    scales_ref,
    gate_hbm,
    up_hbm,
    down_hbm,
    out_ref,
    gate_buf,
    up_buf,
    down_buf,
    row_out,
    row_in,
    route_out,
    route_in,
    rows_f32,
    route_t,
    lines,
    part_out,
    part_in,
    units,
    values,
    mixed,
    back_out,
    back_in,
    gate_sem,
    up_sem,
    down_sem,
    part_send,
    part_recv,
    plain_sem,
    back_send,
    back_recv,
):
    n_ep, n_tp, capacity = sizes
    peers = n_ep * n_tp
    ep = lax.axis_index("ep")
    tp = lax.axis_index("tp")
    me = ep * n_tp + tp
    held = gate_hbm.shape[0]
    unit_ring = gate_buf.shape[0]
    chunks, chunk = down_buf.shape[0], down_buf.shape[3]
    rows = hid_ref.shape[0]
    half = row_in.shape[2]
    block = rows * n_tp
    slots = capacity * n_ep
    ff = gate_hbm.shape[2]
    experts = held * n_ep // 2
    total_rows = n_ep * block

    def unit_copies(j, slot):
        return (
            pltpu.make_async_copy(gate_hbm.at[j], gate_buf.at[slot], gate_sem.at[slot]),
            pltpu.make_async_copy(up_hbm.at[j], up_buf.at[slot], up_sem.at[slot]),
        )

    def down_copy(c):
        return pltpu.make_async_copy(
            down_hbm.at[:, :, pl.ds(c * chunk, chunk)], down_buf.at[c], down_sem.at[c]
        )

    for j in range(unit_ring):
        for copy in unit_copies(j, j):
            copy.start()
    for c in range(chunks):
        down_copy(c).start()

    barrier = pltpu.get_barrier_semaphore()

    def peer_of(offset):
        peer = lax.rem(me + offset, peers)
        return {"ep": peer // n_tp, "tp": lax.rem(peer, n_tp)}, peer

    @pl.loop(1, peers)
    def _(offset):
        where, _peer = peer_of(offset)
        pl.semaphore_signal(barrier, inc=1, device_id=where, device_id_type=MESH)

    route = routing(ids_ref, weights_ref, experts, capacity)
    route_out[...] = route
    route_in[ep] = route
    rotated = rotate(hid_ref, gain_ref, left_ref, right_ref, n_tp).astype(jnp.float32)
    for h in range(n_tp):
        row_out[h] = rotated[h * rows : (h + 1) * rows].astype(jnp.bfloat16)
    row_in[me] = row_out[tp]

    pl.semaphore_wait(barrier, peers - 1)

    @pl.loop(1, n_ep)
    def _(offset):
        pltpu.make_async_remote_copy(
            src_ref=route_out,
            dst_ref=route_in.at[ep],
            send_sem=plain_sem.at[0],
            recv_sem=plain_sem.at[1],
            device_id={"ep": lax.rem(ep + offset, n_ep), "tp": tp},
            device_id_type=MESH,
        ).start()

    @pl.loop(1, peers)
    def _(offset):
        where, peer = peer_of(offset)
        pltpu.make_async_remote_copy(
            src_ref=row_out.at[lax.rem(peer, n_tp)],
            dst_ref=row_in.at[me],
            send_sem=plain_sem.at[2],
            recv_sem=plain_sem.at[3],
            device_id=where,
            device_id_type=MESH,
        ).start()

    def drain(ref, count, sem):
        view = ref.at[pl.ds(0, count)]
        pltpu.make_async_copy(view, view, sem).wait()

    drain(route_in, n_ep - 1, plain_sem.at[1])
    route_t[...] = route_in[...].reshape(total_rows, capacity * experts).T
    first = lax.rem(ep * held, experts)
    owner = (iota((n_ep, total_rows), 1) // block == iota((n_ep, total_rows), 0)).astype(jnp.float32)
    picks = []
    for c in range(capacity):
        line = route_t[pl.ds(c * experts + first, held), :]
        picks.append((line[:, None, :] * owner[None, :, :])[:, None])
    weighted = jnp.concatenate(picks, axis=1).reshape(held * slots, total_rows)
    chosen = jnp.where(weighted > 0.0, 1.0, 0.0).astype(jnp.bfloat16)
    mixing = weighted.T.astype(jnp.bfloat16)

    drain(row_in, peers - 1, plain_sem.at[3])

    @pl.loop(0, n_ep)
    def _(b):
        both = [row_in[b * n_tp + h].astype(jnp.float32) for h in range(n_tp)]
        rows_f32[pl.ds(pl.multiple_of(b * block, block), block), :] = jnp.concatenate(both, axis=0)

    lines[...] = (
        jnp.dot(chosen, rows_f32[...].astype(jnp.bfloat16), preferred_element_type=jnp.float32)
        .astype(jnp.bfloat16)
        .reshape(lines.shape)
    )

    def part_copy(j):
        return pltpu.make_async_remote_copy(
            src_ref=part_out.at[j],
            dst_ref=part_in.at[j],
            send_sem=part_send.at[j],
            recv_sem=part_recv.at[j],
            device_id={"ep": ep, "tp": 1 - tp},
            device_id_type=MESH,
        )

    def project(t, slot):
        line = lines[t]
        gate = jnp.dot(line, gate_buf[slot], preferred_element_type=jnp.float32)
        up = jnp.dot(line, up_buf[slot], preferred_element_type=jnp.float32)
        return gate, up

    def send(t, gate, up):
        part_out[t, :, pl.ds(0, ff)] = gate
        part_out[t, :, pl.ds(ff, ff)] = up
        part_copy(t).start()

    def activate(j):
        scale = scales_ref[j]
        gate = (part_out[j, :, pl.ds(0, ff)] + part_in[j, :, pl.ds(0, ff)]) * scale[0:1]
        up = (part_out[j, :, pl.ds(ff, ff)] + part_in[j, :, pl.ds(ff, ff)]) * scale[1:2]
        units[j] = (gate / (1.0 + jnp.exp(-gate)) * up).astype(jnp.bfloat16)

    def refill(t, slot):
        @pl.when(t + unit_ring < held)
        def _():
            for copy in unit_copies(t + unit_ring, slot):
                copy.start()

    lag = min(LAG, held)

    @pl.loop(0, lag)
    def _(t):
        for copy in unit_copies(t, t):
            copy.wait()
        send(t, *project(t, t))
        refill(t, t)

    @pl.loop(lag, held)
    def _(t):
        slot = lax.rem(t, unit_ring)
        for copy in unit_copies(t, slot):
            copy.wait()
        part_copy(t - lag).wait_recv()
        activate(t - lag)
        send(t, *project(t, slot))
        refill(t, slot)

    for j in range(held - lag, held):
        part_copy(j).wait_recv()
        activate(j)

    def back_copy(c, offset):
        where, peer = peer_of(offset)
        return pltpu.make_async_remote_copy(
            src_ref=back_out.at[c, peer],
            dst_ref=back_in.at[c, me],
            send_sem=back_send.at[c],
            recv_sem=back_recv.at[c],
            device_id=where,
            device_id_type=MESH,
        )

    @pl.loop(0, chunks)
    def _(c):
        down_copy(c).wait()
        for j in range(held):
            values[j * slots : (j + 1) * slots] = jnp.dot(
                units[j], down_buf[c, j], preferred_element_type=jnp.float32
            ).astype(jnp.bfloat16)
        mixed[...] = jnp.dot(mixing, values[...], preferred_element_type=jnp.float32)

        @pl.loop(0, n_ep)
        def _(b):
            both = mixed[pl.ds(pl.multiple_of(b * block, block), block), :]
            for h in range(n_tp):
                back_out[c, b * n_tp + h] = both[h * rows : (h + 1) * rows].astype(jnp.bfloat16)

        @pl.loop(1, peers)
        def _(offset):
            back_copy(c, offset).start()

        back_in[c, me] = back_out[c, me]

    @pl.loop(0, held)
    def _(j):
        part_copy(j).wait_send()

    drain(route_in, n_ep - 1, plain_sem.at[0])
    drain(row_in, peers - 1, plain_sem.at[2])
    for c in range(chunks):
        drain(back_in.at[c], peers - 1, back_recv.at[c])
        for h in range(n_tp):

            def add(e, total):
                return total + back_in[c, e * n_tp + h].astype(jnp.float32)

            total = lax.fori_loop(0, n_ep, add, jnp.zeros((rows, chunk), jnp.float32))
            start = h * half + c * chunk
            out_ref[:, start : start + chunk] = total.astype(jnp.bfloat16)
    for c in range(chunks):
        drain(back_in.at[c], peers - 1, back_send.at[c])


def body(
    hidden,
    norm_gain,
    rot_left,
    rot_right,
    expert_ids,
    gate_weights,
    w_gate,
    w_up,
    w_down,
    unit_scales,
):
    n_ep, n_tp = lax.axis_size("ep"), lax.axis_size("tp")
    peers = n_ep * n_tp
    rows, width = hidden.shape
    group_rows, choices = expert_ids.shape
    held, half, ff = w_gate.shape
    experts = held * n_ep // 2
    capacity = 5 * group_rows * choices // (2 * experts)
    slots = capacity * n_ep
    total_rows = n_ep * group_rows
    unit_ring = min(UNIT_RING, held)
    chunk = min(CHUNK, half)
    chunks = half // chunk
    vmem = pl.BlockSpec(memory_space=pltpu.VMEM)
    hbm = pl.BlockSpec(memory_space=pl.ANY)
    return pl.pallas_call(
        functools.partial(kernel, (n_ep, n_tp, capacity)),
        out_shape=jax.ShapeDtypeStruct((rows, width), jnp.bfloat16),
        in_specs=[vmem] * 7 + [hbm] * 3,
        out_specs=vmem,
        scratch_shapes=[
            pltpu.VMEM((unit_ring, half, ff), jnp.bfloat16),
            pltpu.VMEM((unit_ring, half, ff), jnp.bfloat16),
            pltpu.VMEM((chunks, held, ff, chunk), jnp.bfloat16),
            pltpu.VMEM((n_tp, rows, half), jnp.bfloat16),
            pltpu.VMEM((peers, rows, half), jnp.bfloat16),
            pltpu.VMEM((group_rows, capacity * experts), jnp.float32),
            pltpu.VMEM((n_ep, group_rows, capacity * experts), jnp.float32),
            pltpu.VMEM((total_rows, half), jnp.float32),
            pltpu.VMEM((capacity * experts, total_rows), jnp.float32),
            pltpu.VMEM((held, slots, half), jnp.bfloat16),
            pltpu.VMEM((held, slots, 2 * ff), jnp.float32),
            pltpu.VMEM((held, slots, 2 * ff), jnp.float32),
            pltpu.VMEM((held, slots, ff), jnp.bfloat16),
            pltpu.VMEM((held * slots, chunk), jnp.bfloat16),
            pltpu.VMEM((total_rows, chunk), jnp.float32),
            pltpu.VMEM((chunks, peers, rows, chunk), jnp.bfloat16),
            pltpu.VMEM((chunks, peers, rows, chunk), jnp.bfloat16),
            pltpu.SemaphoreType.DMA((unit_ring,)),
            pltpu.SemaphoreType.DMA((unit_ring,)),
            pltpu.SemaphoreType.DMA((chunks,)),
            pltpu.SemaphoreType.DMA((held,)),
            pltpu.SemaphoreType.DMA((held,)),
            pltpu.SemaphoreType.DMA((4,)),
            pltpu.SemaphoreType.DMA((chunks,)),
            pltpu.SemaphoreType.DMA((chunks,)),
        ],
        compiler_params=pltpu.CompilerParams(
            collective_id=0, has_side_effects=True, vmem_limit_bytes=63 * 1024 * 1024
        ),
    )(
        hidden,
        norm_gain.reshape(1, width),
        rot_left,
        rot_right,
        expert_ids,
        gate_weights,
        unit_scales,
        w_gate,
        w_up,
        w_down,
    )


def solution(mesh):
    placed = (
        P(("groups", "ep", "tp"), None),
        P(),
        P(),
        P(),
        P(("groups", "ep"), None),
        P(("groups", "ep"), None),
        P("ep", "tp", None),
        P("ep", "tp", None),
        P("ep", None, "tp"),
        P("ep", None, None),
    )
    return jax.shard_map(
        body, mesh=mesh, in_specs=placed, out_specs=P(("groups", "ep", "tp"), None), check_vma=False
    )
```
